256 devices in a mesh: dp: 4 (over y), expert: 32 (over x, z), tensor: 2 (over core).
Axes of the slice: x: 4, y: 4, z: 8, core: 2. Of those that a mesh axis runs over, the one named last changes fastest.
Arguments:
- tokens: bfloat16 [16384, 4096], P(('dp', 'expert')), may hold values from -6 to 6
- cotangent: bfloat16 [16384, 4096], P(('dp', 'expert')), may hold values from -6 to 6
- routes: int32 [16384, 1], P(('dp', 'expert')), may hold values from 0 to 31; in each aligned block of 128 rows (0 to 127, 128 to 255, ...) at most 6 rows name the same one
- cluster: int32 [32, 512], replicated, may hold values from -1 to 14783, as said below
- w_gate: bfloat16 [14784, 4096], P(('expert', 'tensor'), 'dp'), may hold values from -0.09375 to 0.09375
- w_up: bfloat16 [14784, 4096], P(('expert', 'tensor'), 'dp'), may hold values from -0.09375 to 0.09375
- w_down: bfloat16 [14784, 4096], P(('expert', 'tensor'), 'dp'), may hold values from -0.25 to 0.25
Outputs:
- layer_out: bfloat16 [16384, 4096], P(('dp', 'expert'))
- grad_tokens: bfloat16 [16384, 4096], P(('dp', 'expert'))
The draws below stay inside these ranges and needn't reach their ends.
Inputs may be any that keep to these rules, and one draw needn't show every extreme that they name: `routes`: in each aligned block of 128 rows no expert is named more than 6 times, and some block names one expert exactly 6 times; every expert is named somewhere. `cluster`: every neuron appears exactly once and each expert has 462 live slots. Slot j = q * 256 + s * 4 + k (k below 4) holds -1 or a neuron of source shard s, that is a row from s * 231 to (s + 1) * 231 - 1; shard s fills exactly 4 such slots of some experts' halves and fewer of others.
All inputs are finite; a program needn't handle non-finite values.
Results may differ from the reference program's by a relative error of at most 0.0059.
Values may be sent and summed in bfloat16 or wider, within the bound.
A program may use at most 128 MiB of HBM per device.

```python
import math
import jax
import jax.numpy as jnp
import numpy as np
from jax import lax

D = 4096
LIVE = 462
SLOTS = 512
TOK_DEV = 128
EXPERTS = 32
FFW = 14784
CAP = 6
TOKENS = 16384
N_DP = 4
N_EXPERT = 32
N_TENSOR = 2


def draw_cluster(key, part):
    shards = N_EXPERT * N_TENSOR
    half_slots = SLOTS // N_TENSOR
    per_shard = half_slots // shards
    live_half = LIVE // N_TENSOR
    offset = jax.random.randint(jax.random.fold_in(key, 11), (), 0, half_slots)
    dest = jnp.arange(shards, dtype=jnp.int32)[:, None, None]
    source = jnp.arange(shards, dtype=jnp.int32)[None, :, None]
    within = jnp.arange(per_shard, dtype=jnp.int32)[None, None, :]
    place = (per_shard * (dest + source) + within + offset) % half_slots
    keys = jax.random.split(jax.random.fold_in(key, 23), shards)
    orders = jax.vmap(lambda single: jax.random.permutation(single, live_half))(keys).astype(jnp.int32)
    source_full = jnp.broadcast_to(source, place.shape)
    clipped = jnp.minimum(place, live_half - 1)
    neuron = source_full * live_half + orders[source_full, clipped]
    chosen = jnp.where(place < live_half, neuron, -1)
    return chosen.reshape(N_EXPERT, SLOTS).astype(jnp.int32)


def level_of(rng, extent, pieces, least, top_value):
    def one(axis_at, blocks):
        steps = jax.random.uniform(jax.random.fold_in(jax.random.fold_in(rng, 6), axis_at), (blocks,), jnp.float32, least / len(pieces), top_value / len(pieces))
        return jnp.repeat(jnp.exp(steps), extent[axis_at] // blocks).reshape((-1,) + (1,) * (len(extent) - axis_at - 1))

    level = one(*pieces[0])
    for cut in pieces[1:]:
        level = level * one(*cut)
    return level


def shared_out(key, own, number, rows, count, top, most, slope):
    sequence = jax.random.permutation(key, count)
    crowded, ordinary = shares(count, rows * top, most, slope, True), shares(count, rows * top, most, slope, False)
    places = jnp.arange(count)

    def named(sizes, rotation):
        used = int((sizes > 0).sum())
        fixed = max(1, used // 4)
        shifted = fixed + (places - fixed + rotation * (used - fixed)) % max(1, count - fixed)
        return jnp.zeros((count,), jnp.int32).at[sequence[jnp.where(places < fixed, places, shifted)]].set(jnp.asarray(sizes, jnp.int32))

    sizes = jnp.where(number % 4 == 0, named(crowded, number // 4), named(ordinary, number - number // 4 - 1))
    mixed = jax.random.permutation(jax.random.fold_in(own, 3), count)
    giver, receiver = mixed[0:count // 2 * 2:2], mixed[1:count // 2 * 2:2]
    room = jnp.minimum(sizes[giver] - 1, most - sizes[receiver]) // 2
    room = jnp.where((giver == sequence[0]) | (receiver == sequence[0]) | (sizes[receiver] == 0), 0, jnp.maximum(room, 0))
    shifted = jax.random.randint(jax.random.fold_in(own, 4), (count // 2,), 0, 1 << 20) % (room + 1)
    sizes = sizes.at[giver].add(-shifted).at[receiver].add(shifted)
    labels = jnp.searchsorted(jnp.cumsum(sizes), jnp.arange(rows * top), side="right").astype(jnp.int32)
    listing = labels.reshape(top, rows).T
    listing = listing[jax.random.permutation(jax.random.fold_in(own, 1), rows)]
    rotation = jax.random.randint(jax.random.fold_in(own, 2), (rows, 1), 0, top)
    return jnp.take_along_axis(listing, (jnp.arange(top)[None, :] + rotation) % top, axis=1)


def shares(number_of, total, reach, lean, full):
    loads = [(1 << 20) // math.isqrt(standing ** lean) + 1 for standing in range(1, number_of + 1)]
    largest = reach if full else min(reach, max(-(-total // number_of), total * loads[0] // sum(loads)))
    least = 1 if total - largest >= number_of - 1 else 0
    holding, surplus = [largest] + [least] * (number_of - 1), total - largest - least * (number_of - 1)
    while surplus > 0:
        free = [i for i in range(1, number_of) if holding[i] < largest] or [i for i in range(1, number_of) if holding[i] < reach]
        mass, left = sum([loads[i] for i in free]), surplus
        for i in free:
            addition = min(reach - holding[i], max(1, left * loads[i] // mass), surplus)
            holding[i] = holding[i] + addition
            surplus = surplus - addition
    return np.array(holding)


def centred(stream_key, extent, width, bound, cuts=(), kind=jnp.bfloat16):
    result = width * jax.random.normal(stream_key, extent, jnp.float32)
    if cuts:
        result = result * level_of(stream_key, extent, cuts, -0.22, 0.18)
    return jnp.clip(result, -bound, bound).astype(kind)


def setup_inputs(seed: int = 0) -> dict:
    key_of = jax.random.split(jax.random.key(seed), 8)
    tokens = centred(key_of[0], (TOKENS, D), 1.0, 6.0, ((0, 128),))
    cotangent = centred(key_of[1], (TOKENS, D), 1.0, 6.0, ((0, 128),))
    routes_keys = jax.random.split(jax.random.fold_in(key_of[2], 1), TOKENS // TOK_DEV)
    routes_turns = jax.random.permutation(jax.random.fold_in(key_of[2], 3), TOKENS // TOK_DEV)
    routes = jax.vmap(lambda own, number: shared_out(jax.random.fold_in(key_of[2], 2), own, number, TOK_DEV, EXPERTS, 1, CAP, 2))(routes_keys, routes_turns).reshape((TOKENS, 1))
    cluster = draw_cluster(jax.random.fold_in(key_of[7], 71), 0)
    w_gate = centred(key_of[4], (FFW, D), D ** -0.5, 0.09375, ((0, 64), (1, 4)))
    w_up = centred(key_of[5], (FFW, D), D ** -0.5, 0.09375, ((0, 64), (1, 4)))
    w_down = centred(key_of[6], (FFW, D), LIVE ** -0.5, 0.25, ((0, 64), (1, 4)))
    return {"tokens": tokens, "cotangent": cotangent, "routes": routes, "cluster": cluster, "w_gate": w_gate, "w_up": w_up, "w_down": w_down}


def expert_pass(x_rows, dy_rows, picks, w_gate, w_up, w_down):
    is_live = (picks >= 0)[:, None]
    safe_rows = jnp.clip(picks, 0, w_gate.shape[0] - 1).astype(jnp.int32)
    zero_row = jnp.zeros((), w_gate.dtype)
    gate_rows = jnp.where(is_live, w_gate[safe_rows], zero_row)
    up_rows = jnp.where(is_live, w_up[safe_rows], zero_row)
    down_rows = jnp.where(is_live, w_down[safe_rows], zero_row)
    half_slots = picks.shape[0] // N_TENSOR
    out_sum = jnp.zeros((x_rows.shape[0], x_rows.shape[1]), jnp.float32)
    grad_sum = jnp.zeros((x_rows.shape[0], x_rows.shape[1]), jnp.float32)
    for quarter in range(N_TENSOR):
        lower = quarter * half_slots
        gate_w = gate_rows[lower:lower + half_slots]
        up_w = up_rows[lower:lower + half_slots]
        down_w = down_rows[lower:lower + half_slots]
        pre_gate = jnp.dot(x_rows, gate_w.T, preferred_element_type=jnp.float32)
        pre_up = jnp.dot(x_rows, up_w.T, preferred_element_type=jnp.float32)
        sig_gate = jax.nn.sigmoid(pre_gate)
        hidden = (pre_gate * sig_gate * pre_up).astype(jnp.bfloat16)
        out_part = jnp.dot(hidden, down_w, preferred_element_type=jnp.float32).astype(jnp.bfloat16)
        out_part = lax.optimization_barrier(out_part)
        out_sum = out_sum + out_part.astype(jnp.float32)
        grad_hidden = jnp.dot(dy_rows, down_w.T, preferred_element_type=jnp.float32)
        grad_gate = (grad_hidden * pre_up * sig_gate * (1.0 + pre_gate * (1.0 - sig_gate))).astype(jnp.bfloat16)
        grad_up = (grad_hidden * pre_gate * sig_gate).astype(jnp.bfloat16)
        grad_part = jnp.dot(grad_gate, gate_w, preferred_element_type=jnp.float32)
        grad_part = grad_part + jnp.dot(grad_up, up_w, preferred_element_type=jnp.float32)
        grad_part = lax.optimization_barrier(grad_part.astype(jnp.bfloat16))
        grad_sum = grad_sum + grad_part.astype(jnp.float32)
    return out_sum.astype(jnp.bfloat16), grad_sum.astype(jnp.bfloat16)


def reference(tokens, cotangent, routes, cluster, w_gate, w_up, w_down):
    blocks = N_DP * N_EXPERT
    expert_of = routes[:, 0].reshape(blocks, TOK_DEV)
    onehot = (expert_of[:, :, None] == jnp.arange(N_EXPERT, dtype=jnp.int32)[None, None, :]).astype(jnp.int32)
    position = jnp.sum((jnp.cumsum(onehot, axis=1) - 1) * onehot, axis=2)
    block_ids = jnp.arange(blocks, dtype=jnp.int32)[:, None]
    row_ids = (block_ids * CAP + position).reshape(-1).astype(jnp.int32)
    flat_expert = expert_of.reshape(-1).astype(jnp.int32)
    empty = jnp.zeros((N_EXPERT, blocks * CAP, D), jnp.bfloat16)
    x_buffer = empty.at[flat_expert, row_ids].set(tokens)
    dy_buffer = empty.at[flat_expert, row_ids].set(cotangent)

    def one_expert(items):
        return expert_pass(items[0], items[1], items[2], w_gate, w_up, w_down)

    out_buffer, grad_buffer = lax.map(one_expert, (x_buffer, dy_buffer, cluster))
    layer_out = out_buffer[flat_expert, row_ids]
    grad_tokens = grad_buffer[flat_expert, row_ids]
    return (layer_out, grad_tokens)
```

```python
import functools

import jax
import jax.numpy as jnp
from jax import lax
from jax.experimental import pallas as pl
from jax.experimental.pallas import tpu as pltpu
from jax.sharding import PartitionSpec as P

NX, NZ = 4, 8
NE = NX * NZ
NDP = 4
CAP = 6
TILES = 3
CHUNKS = 2
PER = NE // CHUNKS
COLS = 1024
STEP = 512
LAG = 4
MESH = pl.DeviceIdType.MESH
BF = jnp.bfloat16
F32 = jnp.float32


def iota(shape, dim):
    return lax.broadcasted_iota(jnp.int32, shape, dim)


def onehot(mask):
    return jnp.where(mask, 1.0, 0.0).astype(BF)


def dot(a, b):
    return jnp.dot(a, b, preferred_element_type=F32)


def dot_t(a, b):
    return lax.dot_general(a, b, (((1,), (1,)), ((), ())), preferred_element_type=F32)


def displacement(i):
    j, k = i // NZ, lax.rem(i, NZ)
    dx = lax.rem(j, 2) * 2 + j // 2
    odd, half = lax.rem(k, 2), (k + 1) // 2
    dz = lax.rem(odd * half + (1 - odd) * (NZ - half), NZ)
    return dx, dz


def kernel(
    tok_ref,
    cot_ref,
    routes_ref,
    cluster_ref,
    wg_ref,
    wu_ref,
    wd_ref,
    out_ref,
    grad_ref,
    sel,
    ws,
    wr,
    ts,
    tr,
    xd,
    pre,
    ps,
    pr,
    own,
    ob,
    rs,
    hr,
    perm_in,
    perm_out,
    local_sem,
    w_send,
    w_recv,
    y_send,
    y_recv,
    t_send,
    t_recv,
    tf_send,
    tf_recv,
    p_send,
    p_recv,
    r_send,
    r_recv,
    rf_send,
    rf_recv,
):
    dp = lax.axis_index("dp")
    me = lax.axis_index("expert")
    core = lax.axis_index("tensor")
    mx, mz = me // NZ, lax.rem(me, NZ)
    shard = me * 2 + core
    rows_dev = wg_ref.shape[0]
    n_tok = tok_ref.shape[0]
    partner = (dp, me, 1 - core)

    def ahead(i):
        dx, dz = displacement(i)
        return lax.rem(mx + dx, NX) * NZ + lax.rem(mz + dz, NZ)

    def behind(i):
        dx, dz = displacement(i)
        return lax.rem(mx + NX - dx, NX) * NZ + lax.rem(mz + NZ - dz, NZ)

    def plane(step):
        return lax.rem(dp + NDP + step, NDP)

    def loop(lower, upper, body):
        def run(i, carry):
            body(i)
            return carry

        lax.fori_loop(lower, upper, run, 0)

    barrier = pltpu.get_barrier_semaphore()

    def greet(i):
        pl.semaphore_signal(barrier, 1, device_id=(dp, ahead(i), core), device_id_type=MESH)

    loop(1, NE, greet)
    pl.semaphore_signal(barrier, 1, device_id=(plane(1), me, core), device_id_type=MESH)
    pl.semaphore_signal(barrier, 1, device_id=(plane(-1), me, core), device_id_type=MESH)
    pl.semaphore_signal(barrier, 1, device_id=partner, device_id_type=MESH)

    half_slots = cluster_ref.shape[1] // 2
    sub = iota((8, 1), 0)
    slot = (sub // 4) * half_slots + shard * 4 + lax.rem(sub, 4)
    lanes = iota((8, cluster_ref.shape[1]), 1)
    neuron = iota((8, rows_dev), 1) + shard * rows_dev
    for e in range(NE):
        line = jnp.broadcast_to(cluster_ref[e : e + 1, :], lanes.shape)
        pick = jnp.sum(jnp.where(lanes == slot, line, 0), axis=1, keepdims=True)
        sel[e * 8 : e * 8 + 8, :] = jnp.where(neuron == pick, 1.0, 0.0)
    chosen = sel[...].astype(BF)
    for a, weight in enumerate((wg_ref, wu_ref, wd_ref)):
        for j in range(COLS // STEP):
            cols = slice(j * STEP, (j + 1) * STEP)
            ws.at[a].reshape(NE * 8, COLS)[:, cols] = dot(chosen, weight[:, cols]).astype(BF)

    pl.semaphore_wait(barrier, NE - 1 + 3)

    def weight_copy(i):
        return pltpu.make_async_remote_copy(
            src_ref=ws.at[:, ahead(i)],
            dst_ref=wr.at[dp, :, i],
            send_sem=w_send.at[i],
            recv_sem=w_recv.at[i],
            device_id=(dp, ahead(i), core),
            device_id_type=MESH,
        )

    own_weights = pltpu.make_async_copy(ws.at[:, me], wr.at[dp, :, 0], local_sem.at[0])
    own_weights.start()
    loop(1, NE, lambda i: weight_copy(i).start())

    square = (n_tok, n_tok)
    by_lane = jnp.broadcast_to(routes_ref[...], square)
    eye = iota(square, 0) == iota(square, 1)
    route_col = jnp.sum(jnp.where(eye, by_lane, 0), axis=1, keepdims=True)
    same = by_lane == route_col
    place_row = jnp.sum(
        jnp.where(same & (iota(square, 0) < iota(square, 1)), 1, 0), axis=0, keepdims=True
    )
    place_col = jnp.sum(
        jnp.where(same & (iota(square, 1) < iota(square, 0)), 1, 0), axis=1, keepdims=True
    )
    route_row = routes_ref[...]

    tall = (NE * 8, n_tok)
    row = iota(tall, 0)
    row_expert, row_sub = row // 8, lax.rem(row, 8)
    mine = row_expert == route_row
    for t in range(TILES):
        lhs = [onehot(mine & (place_row == row_sub + 8 * t - CAP * (t + j))) for j in range(2)]
        for c in range(COLS // STEP):
            total = None
            for j in range(2):
                block, source = (t + j) // 2, (tok_ref, cot_ref)[(t + j) % 2]
                first = pl.multiple_of(core * 2 * COLS + block * COLS + c * STEP, STEP)
                term = dot(lhs[j], source[:, pl.ds(first, STEP)])
                total = term if total is None else total + term
            ts.at[t].reshape(NE * 8, COLS)[:, c * STEP : (c + 1) * STEP] = total.astype(BF)

    def token_copy(i):
        return pltpu.make_async_remote_copy(
            src_ref=ts.at[:, ahead(i)],
            dst_ref=tr.at[core, i // PER, :, lax.rem(i, PER)],
            send_sem=t_send.at[i],
            recv_sem=t_recv.at[i],
            device_id=(dp, ahead(i), core),
            device_id_type=MESH,
        )

    own_tokens = pltpu.make_async_copy(ts.at[:, me], tr.at[core, 0, :, 0], local_sem.at[1])
    own_tokens.start()
    loop(1, NE, lambda i: token_copy(i).start())

    wide = (2 * CAP * PER, 2 * 8 * PER)
    r, q = iota(wide, 0), iota(wide, 1)
    a = jnp.where(r >= CAP * PER, 1, 0)
    t = jnp.where(q >= 8 * PER, 1, 0)
    r = r - a * (CAP * PER)
    q = q - t * (8 * PER)
    for h in range(2):
        p = lax.rem(q, 8) + 8 * (t + h) - CAP * (2 * h + a)
        perm_in[h] = onehot((p >= 0) & (p < CAP) & (r == CAP * (q // 8) + p))
    wide = (8 * PER, 2 * CAP * PER)
    r, q = iota(wide, 0), iota(wide, 1)
    j = jnp.where(q >= CAP * PER, 1, 0)
    q = q - j * (CAP * PER)
    for t in range(TILES):
        p = 2 * t + lax.rem(r, 8) - CAP * j
        perm_out[t] = onehot((p >= 0) & (p < CAP) & (q == CAP * (r // 8) + p))

    def plane_copy(i, which, step, slot_sem):
        return pltpu.make_async_remote_copy(
            src_ref=wr.at[which, :, i],
            dst_ref=wr.at[which, :, i],
            send_sem=y_send.at[slot_sem, i],
            recv_sem=y_recv.at[slot_sem, i],
            device_id=(plane(step), me, core),
            device_id_type=MESH,
        )

    def relay_copy(i):
        sign = 1 - 2 * lax.rem(i, 2)
        return plane_copy(i, plane(-sign), sign, 2)

    def spread(i):
        plane_copy(i, dp, 1, 0).start()
        plane_copy(i, dp, -1, 1).start()

    def relay(i):
        plane_copy(i, plane(-1), 1, 0).wait_recv()
        plane_copy(i, plane(1), -1, 1).wait_recv()
        relay_copy(i).start()

    own_weights.wait()
    spread(0)

    def weight_step(i):
        weight_copy(i).wait_recv()
        spread(i)

        @pl.when(i >= LAG)
        def _():
            relay(i - LAG)

    loop(1, NE, weight_step)
    loop(NE - LAG, NE, relay)

    def token_forward(i):
        return pltpu.make_async_remote_copy(
            src_ref=tr.at[core, i // PER, :, lax.rem(i, PER)],
            dst_ref=tr.at[core, i // PER, :, lax.rem(i, PER)],
            send_sem=tf_send.at[i],
            recv_sem=tf_recv.at[i],
            device_id=partner,
            device_id_type=MESH,
        )

    def token_step(i):
        token_copy(i).wait_recv()
        token_forward(i).start()

    own_tokens.wait()
    token_forward(0).start()
    loop(1, PER, token_step)
    loop(0, NE, lambda i: relay_copy(i).wait_recv())

    def return_copy(i):
        return pltpu.make_async_remote_copy(
            src_ref=rs.at[i // PER, :, lax.rem(i, PER)],
            dst_ref=hr.at[core, :, me],
            send_sem=r_send.at[i],
            recv_sem=r_recv.at[i],
            device_id=(dp, behind(i), core),
            device_id_type=MESH,
        )

    own_result = pltpu.make_async_copy(rs.at[0, :, 0], hr.at[core, :, me], local_sem.at[2])
    rows = CAP * PER
    for n in range(CHUNKS):
        if n:
            loop(n * PER, (n + 1) * PER, token_step)
        loop(n * PER, (n + 1) * PER, lambda i: token_forward(i).wait_recv())

        def unpack(b):
            half, h = b // 2, lax.rem(b, 2)
            source = tr.at[half, n, pl.ds(h, 2)].reshape(2 * 8 * PER, COLS)
            for c in range(COLS // STEP):
                cols = slice(c * STEP, (c + 1) * STEP)
                xd[b, :, cols] = dot(perm_in[h], source[:, cols]).astype(BF)

        loop(0, 4, unpack)
        pre[...] = jnp.zeros_like(pre)

        def project(b):
            gate_up = wr.at[b, pl.ds(0, 2)].reshape(2 * NE * 8, COLS)
            down = wr.at[b, 2].reshape(NE * 8, COLS)
            pre[:, : 2 * NE * 8] += dot_t(xd[b, :rows], gate_up[...])
            pre[:, 2 * NE * 8 :] += dot_t(xd[b, rows:], down[...])

        loop(0, 4, project)
        width = NE * 8
        gate, up, back = pre[:, :width], pre[:, width : 2 * width], pre[:, 2 * width :]
        s = jax.nn.sigmoid(gate)
        hidden = (gate * s * up).astype(BF)
        grad_gate = (back * up * s * (1.0 + gate * (1.0 - s))).astype(BF)
        grad_up = (back * gate * s).astype(BF)
        grads = jnp.concatenate([grad_gate, grad_up], axis=1)

        def part(b, put):
            gate_up = wr.at[b, pl.ds(0, 2)].reshape(2 * NE * 8, COLS)
            down = wr.at[b, 2].reshape(NE * 8, COLS)
            for c in range(COLS // STEP):
                cols = slice(c * STEP, (c + 1) * STEP)
                put(slice(0, rows), cols, dot(hidden, down[:, cols]))
                put(slice(rows, 2 * rows), cols, dot(grads, gate_up[:, cols]))

        def part_copy(h):
            return pltpu.make_async_remote_copy(
                src_ref=ps.at[n, h],
                dst_ref=pr.at[n, h],
                send_sem=p_send.at[n, h],
                recv_sem=p_recv.at[n, h],
                device_id=partner,
                device_id_type=MESH,
            )

        for h in range(2):

            def put_sent(at, cols, value):
                ps[n, h, at, cols] = value.astype(BF)

            part((1 - core) * 2 + h, put_sent)
            part_copy(h).start()
        for h in range(2):

            def put_own(at, cols, value):
                own[h, at, cols] = value.astype(BF)

            part(core * 2 + h, put_own)
        for h in range(2):
            part_copy(h).wait_recv()
            ob[h * 2 * rows : (h + 1) * 2 * rows, :] = (
                own[h].astype(F32) + pr[n, h].astype(F32)
            ).astype(BF)
        for t in range(TILES):
            for c in range(COLS // STEP):
                cols = slice(c * STEP, (c + 1) * STEP)
                moved = dot(perm_out[t], ob[t * rows : (t + 2) * rows, cols])
                rs.at[n, t].reshape(8 * PER, COLS)[:, cols] = moved.astype(BF)
        if n == 0:
            own_result.start()
            loop(1, PER, lambda i: return_copy(i).start())
        else:
            loop(n * PER, (n + 1) * PER, lambda i: return_copy(i).start())

    def result_forward(i):
        at = ahead(i)
        return pltpu.make_async_remote_copy(
            src_ref=hr.at[core, :, at],
            dst_ref=hr.at[core, :, at],
            send_sem=rf_send.at[i],
            recv_sem=rf_recv.at[i],
            device_id=partner,
            device_id_type=MESH,
        )

    def result_step(i):
        return_copy(i).wait_recv()
        result_forward(i).start()

    own_result.wait()
    result_forward(0).start()
    loop(1, NE, result_step)
    loop(0, NE, lambda i: result_forward(i).wait_recv())

    long = (n_tok, 2 * NE * 8)
    q = iota(long, 1)
    j = jnp.where(q >= NE * 8, 1, 0)
    q = q - j * (NE * 8)
    here = route_col == q // 8
    for h in range(2):
        table = jnp.concatenate(
            [
                onehot(here & (place_col == lax.rem(q, 8) + 8 * (h + j) - CAP * (2 * h + b)))
                for b in range(2)
            ],
            axis=0,
        )
        for half in range(2):
            source = hr.at[half, pl.ds(h, 2)].reshape(2 * NE * 8, COLS)
            for c in range(COLS // STEP):
                value = dot(table, source[:, c * STEP : (c + 1) * STEP]).astype(BF)
                first = (2 * half + h) * COLS + c * STEP
                out_ref[:, first : first + STEP] = value[:n_tok]
                grad_ref[:, first : first + STEP] = value[n_tok:]

    def drain(i):
        weight_copy(i).wait_send()
        token_copy(i).wait_send()
        return_copy(i).wait_send()

    loop(1, NE, drain)

    def drain_near(i):
        plane_copy(i, dp, 1, 0).wait_send()
        plane_copy(i, dp, -1, 1).wait_send()
        relay_copy(i).wait_send()
        token_forward(i).wait_send()
        result_forward(i).wait_send()

    loop(0, NE, drain_near)
    for n in range(CHUNKS):
        for h in range(2):
            pltpu.make_async_remote_copy(
                src_ref=ps.at[n, h],
                dst_ref=pr.at[n, h],
                send_sem=p_send.at[n, h],
                recv_sem=p_recv.at[n, h],
                device_id=partner,
                device_id_type=MESH,
            ).wait_send()


def per_device(tokens, cotangent, routes, cluster, w_gate, w_up, w_down):
    n_tok, width = tokens.shape
    rows_dev = w_gate.shape[0]
    dma = pltpu.SemaphoreType.DMA
    rows = CAP * PER
    vmem = pl.BlockSpec(memory_space=pltpu.VMEM)
    shape = jax.ShapeDtypeStruct((n_tok, width), BF)
    return pl.pallas_call(
        kernel,
        out_shape=(shape, shape),
        in_specs=[vmem] * 7,
        out_specs=(vmem, vmem),
        scratch_shapes=[
            pltpu.VMEM((NE * 8, rows_dev), F32),
            pltpu.VMEM((3, NE, 8, COLS), BF),
            pltpu.VMEM((NDP, 3, NE, 8, COLS), BF),
            pltpu.VMEM((TILES, NE, 8, COLS), BF),
            pltpu.VMEM((2, CHUNKS, TILES, PER, 8, COLS), BF),
            pltpu.VMEM((4, 2 * rows, COLS), BF),
            pltpu.VMEM((rows, 3 * NE * 8), F32),
            pltpu.VMEM((CHUNKS, 2, 2 * rows, COLS), BF),
            pltpu.VMEM((CHUNKS, 2, 2 * rows, COLS), BF),
            pltpu.VMEM((2, 2 * rows, COLS), BF),
            pltpu.VMEM((4 * rows, COLS), BF),
            pltpu.VMEM((CHUNKS, TILES, PER, 8, COLS), BF),
            pltpu.VMEM((2, TILES, NE, 8, COLS), BF),
            pltpu.VMEM((2, 2 * rows, 2 * 8 * PER), BF),
            pltpu.VMEM((TILES, 8 * PER, 2 * rows), BF),
            dma((3,)),
            dma((NE,)),
            dma((NE,)),
            dma((3, NE)),
            dma((3, NE)),
            dma((NE,)),
            dma((NE,)),
            dma((NE,)),
            dma((NE,)),
            dma((CHUNKS, 2)),
            dma((CHUNKS, 2)),
            dma((NE,)),
            dma((NE,)),
            dma((NE,)),
            dma((NE,)),
        ],
        compiler_params=pltpu.CompilerParams(
            collective_id=0, has_side_effects=True, vmem_limit_bytes=60 << 20
        ),
    )(tokens, cotangent, routes.reshape(1, n_tok), cluster, w_gate, w_up, w_down)


def solution(mesh):
    in_specs = (
        P(("dp", "expert"), None),
        P(("dp", "expert"), None),
        P(("dp", "expert"), None),
        P(),
        P(("expert", "tensor"), "dp"),
        P(("expert", "tensor"), "dp"),
        P(("expert", "tensor"), "dp"),
    )
    out_specs = (P(("dp", "expert"), None), P(("dp", "expert"), None))
    return jax.shard_map(
        per_device, mesh=mesh, in_specs=in_specs, out_specs=out_specs, check_vma=False
    )
```

```python
import functools

import jax
import jax.numpy as jnp
from jax import lax
from jax.experimental import pallas as pl
from jax.experimental.pallas import tpu as pltpu
from jax.sharding import PartitionSpec as P

NX, NZ = 4, 8
NE = NX * NZ
NDP = 4
CAP = 6
TILES = 3
CHUNKS = 2
PER = NE // CHUNKS
COLS = 1024
STEP = 512
GROUP = 4
GROUPS = NE // GROUP
MESH = pl.DeviceIdType.MESH
VMEM_BYTES = 67_043_328 - (2 * TILES * NE * 8 * COLS + 2 * 256 * 512) * 2
BF = jnp.bfloat16
F32 = jnp.float32


def iota(shape, dim):
    return lax.broadcasted_iota(jnp.int32, shape, dim)


def onehot(mask):
    return jnp.where(mask, 1.0, 0.0).astype(BF)


def dot(a, b):
    return jnp.dot(a, b, preferred_element_type=F32)


def dot_t(a, b):
    return lax.dot_general(a, b, (((1,), (1,)), ((), ())), preferred_element_type=F32)


def along_z(k):
    odd, half = lax.rem(k, 2), (k + 1) // 2
    return lax.rem(odd * half + (1 - odd) * (NZ - half), NZ)


def by_z(i):
    return lax.rem(i, NX), along_z(i // NX)


def by_x(i):
    j = i // NZ
    return lax.rem(j, 2) * 2 + j // 2, along_z(lax.rem(i, NZ))


def kernel(
    tok_hbm,
    cot_hbm,
    routes_hbm,
    cluster_hbm,
    wg_hbm,
    wu_hbm,
    wd_hbm,
    hr,
    table,
    tok_ref,
    cot_ref,
    routes_ref,
    cluster_ref,
    w_ref,
    sel,
    ws,
    wr,
    ts,
    tr,
    xd,
    pre,
    ps,
    pr,
    own,
    ob,
    rs,
    perm_in,
    perm_out,
    in_sem,
    local_sem,
    w_send,
    w_recv,
    y_send,
    y_recv,
    t_send,
    t_recv,
    tf_send,
    tf_recv,
    p_send,
    p_recv,
    r_send,
    r_recv,
    rf_send,
    rf_recv,
):
    dp = lax.axis_index("dp")
    me = lax.axis_index("expert")
    core = lax.axis_index("tensor")
    mx, mz = me // NZ, lax.rem(me, NZ)
    shard = me * 2 + core
    rows_dev = w_ref.shape[1]
    n_tok = tok_ref.shape[0]
    partner = (dp, me, 1 - core)

    def ahead(step):
        return lax.rem(mx + step[0], NX) * NZ + lax.rem(mz + step[1], NZ)

    def behind(step):
        return lax.rem(mx + NX - step[0], NX) * NZ + lax.rem(mz + NZ - step[1], NZ)

    def plane(step):
        return lax.rem(dp + NDP + step, NDP)

    def loop(lower, upper, body):
        def run(i, carry):
            body(i)
            return carry

        lax.fori_loop(lower, upper, run, 0)

    barrier = pltpu.get_barrier_semaphore()

    def greet(i):
        pl.semaphore_signal(barrier, 1, device_id=(dp, ahead(by_z(NE - i)), core), device_id_type=MESH)

    loop(1, NE, greet)
    pl.semaphore_signal(barrier, 1, device_id=(plane(1), me, core), device_id_type=MESH)
    pl.semaphore_signal(barrier, 1, device_id=(plane(-1), me, core), device_id_type=MESH)
    pl.semaphore_signal(barrier, 1, device_id=partner, device_id_type=MESH)

    pulls = [
        pltpu.make_async_copy(source, target, in_sem.at[k])
        for k, (source, target) in enumerate(
            (
                (cluster_hbm, cluster_ref),
                (wg_hbm, w_ref.at[0]),
                (wu_hbm, w_ref.at[1]),
                (wd_hbm, w_ref.at[2]),
                (routes_hbm, routes_ref),
                (tok_hbm, tok_ref),
                (cot_hbm, cot_ref),
            )
        )
    ]
    for pull in pulls:
        pull.start()
    pulls[0].wait()

    half_slots = cluster_ref.shape[1] // 2
    sub = iota((8, 1), 0)
    slot = (sub // 4) * half_slots + shard * 4 + lax.rem(sub, 4)
    lanes = iota((8, cluster_ref.shape[1]), 1)
    neuron = iota((8, rows_dev), 1) + shard * rows_dev
    for e in range(NE):
        line = jnp.broadcast_to(cluster_ref[e : e + 1, :], lanes.shape)
        pick = jnp.sum(jnp.where(lanes == slot, line, 0), axis=1, keepdims=True)
        sel[e * 8 : e * 8 + 8, :] = jnp.where(neuron == pick, 1.0, 0.0)
    chosen = sel[...].astype(BF)
    for a in range(3):
        pulls[1 + a].wait()
        for j in range(COLS // STEP):
            cols = slice(j * STEP, (j + 1) * STEP)
            ws.at[a].reshape(NE * 8, COLS)[:, cols] = dot(chosen, w_ref[a, :, cols]).astype(BF)

    pl.semaphore_wait(barrier, NE - 1 + 3)

    def weight_copy(i):
        to = ahead(by_z(i))
        return pltpu.make_async_remote_copy(
            src_ref=ws.at[:, to],
            dst_ref=wr.at[dp, :, i],
            send_sem=w_send.at[0],
            recv_sem=w_recv.at[i // GROUP],
            device_id=(dp, to, core),
            device_id_type=MESH,
        )

    own_weights = pltpu.make_async_copy(ws.at[:, me], wr.at[dp, :, 0], local_sem.at[0])
    own_weights.start()
    loop(1, NE, lambda i: weight_copy(i).start())

    def landed(ref, sem):
        pltpu.make_async_remote_copy(
            src_ref=ref,
            dst_ref=ref,
            send_sem=local_sem.at[3],
            recv_sem=sem,
            device_id=partner,
            device_id_type=MESH,
        ).wait_recv()

    def left(ref, sem):
        pltpu.make_async_remote_copy(
            src_ref=ref,
            dst_ref=ref,
            send_sem=sem,
            recv_sem=local_sem.at[3],
            device_id=partner,
            device_id_type=MESH,
        ).wait_send()

    for pull in pulls[4:]:
        pull.wait()

    square = (n_tok, n_tok)
    by_lane = jnp.broadcast_to(routes_ref[...], square)
    eye = iota(square, 0) == iota(square, 1)
    route_col = jnp.sum(jnp.where(eye, by_lane, 0), axis=1, keepdims=True)
    same = by_lane == route_col
    place_row = jnp.sum(
        jnp.where(same & (iota(square, 0) < iota(square, 1)), 1, 0), axis=0, keepdims=True
    )
    place_col = jnp.sum(
        jnp.where(same & (iota(square, 1) < iota(square, 0)), 1, 0), axis=1, keepdims=True
    )
    route_row = routes_ref[...]

    tall = (NE * 8, n_tok)
    row = iota(tall, 0)
    row_expert, row_sub = row // 8, lax.rem(row, 8)
    mine = row_expert == route_row
    for t in range(TILES):
        lhs = [onehot(mine & (place_row == row_sub + 8 * t - CAP * (t + j))) for j in range(2)]
        for c in range(COLS // STEP):
            total = None
            for j in range(2):
                block, source = (t + j) // 2, (tok_ref, cot_ref)[(t + j) % 2]
                first = pl.multiple_of(core * 2 * COLS + block * COLS + c * STEP, STEP)
                term = dot(lhs[j], source[:, pl.ds(first, STEP)])
                total = term if total is None else total + term
            ts.at[t].reshape(NE * 8, COLS)[:, c * STEP : (c + 1) * STEP] = total.astype(BF)

    def token_copy(i):
        to = ahead(by_x(i))
        return pltpu.make_async_remote_copy(
            src_ref=ts.at[:, to],
            dst_ref=tr.at[core, i // PER, :, lax.rem(i, PER)],
            send_sem=t_send.at[0],
            recv_sem=t_recv.at[i // GROUP],
            device_id=(dp, to, core),
            device_id_type=MESH,
        )

    own_tokens = pltpu.make_async_copy(ts.at[:, me], tr.at[core, 0, :, 0], local_sem.at[1])
    own_tokens.start()
    loop(1, NE, lambda i: token_copy(i).start())

    long = (n_tok, 2 * NE * 8)
    q = iota(long, 1)
    j = jnp.where(q >= NE * 8, 1, 0)
    q = q - j * (NE * 8)
    here = route_col == ahead(by_x(q // 8))
    for h in range(2):
        for b in range(2):
            spot = place_col == lax.rem(q, 8) + 8 * (h + j) - CAP * (2 * h + b)
            table[h, b * n_tok : (b + 1) * n_tok, :] = onehot(here & spot)

    wide = (2 * CAP * PER, 2 * 8 * PER)
    r, q = iota(wide, 0), iota(wide, 1)
    a = jnp.where(r >= CAP * PER, 1, 0)
    t = jnp.where(q >= 8 * PER, 1, 0)
    r = r - a * (CAP * PER)
    q = q - t * (8 * PER)
    for h in range(2):
        p = lax.rem(q, 8) + 8 * (t + h) - CAP * (2 * h + a)
        perm_in[h] = onehot((p >= 0) & (p < CAP) & (r == CAP * (q // 8) + p))
    wide = (8 * PER, 2 * CAP * PER)
    r, q = iota(wide, 0), iota(wide, 1)
    j = jnp.where(q >= CAP * PER, 1, 0)
    q = q - j * (CAP * PER)
    for t in range(TILES):
        p = 2 * t + lax.rem(r, 8) - CAP * j
        perm_out[t] = onehot((p >= 0) & (p < CAP) & (q == CAP * (r // 8) + p))

    def plane_copy(g, which, step, way):
        group = wr.at[which, :, pl.ds(g * GROUP, GROUP)]
        return pltpu.make_async_remote_copy(
            src_ref=group,
            dst_ref=group,
            send_sem=y_send.at[0],
            recv_sem=y_recv.at[way, g],
            device_id=(plane(step), me, core),
            device_id_type=MESH,
        )

    def relay_copy(g):
        sign = 1 - 2 * lax.rem(g, 2)
        return plane_copy(g, plane(-sign), sign, 2)

    def spread(g):
        plane_copy(g, dp, 1, 0).start()
        plane_copy(g, dp, -1, 1).start()

    def relay(g):
        plane_copy(g, plane(-1), 1, 0).wait_recv()
        plane_copy(g, plane(1), -1, 1).wait_recv()
        relay_copy(g).start()

    own_weights.wait()
    landed(wr.at[dp, :, pl.ds(1, GROUP - 1)], w_recv.at[0])
    spread(0)

    def weight_step(g):
        landed(wr.at[dp, :, pl.ds(g * GROUP, GROUP)], w_recv.at[g])
        spread(g)
        relay(g - 1)

    loop(1, GROUPS, weight_step)
    relay(GROUPS - 1)

    def token_group(g):
        per = PER // GROUP
        return tr.at[core, g // per, :, pl.ds(lax.rem(g, per) * GROUP, GROUP)]

    def token_forward(g):
        return pltpu.make_async_remote_copy(
            src_ref=token_group(g),
            dst_ref=token_group(g),
            send_sem=tf_send.at[0],
            recv_sem=tf_recv.at[g // (PER // GROUP)],
            device_id=partner,
            device_id_type=MESH,
        )

    def token_step(g):
        landed(token_group(g), t_recv.at[g])
        token_forward(g).start()

    own_tokens.wait()
    landed(tr.at[core, 0, :, pl.ds(1, GROUP - 1)], t_recv.at[0])
    token_forward(0).start()
    loop(1, PER // GROUP, token_step)
    loop(0, GROUPS, lambda g: relay_copy(g).wait_recv())

    def return_copy(i):
        return pltpu.make_async_remote_copy(
            src_ref=rs.at[i // PER, :, lax.rem(i, PER)],
            dst_ref=hr.at[core, :, i],
            send_sem=r_send.at[0],
            recv_sem=r_recv.at[i // GROUP],
            device_id=(dp, behind(by_x(i)), core),
            device_id_type=MESH,
        )

    own_result = pltpu.make_async_copy(rs.at[0, :, 0], hr.at[core, :, 0], local_sem.at[2])
    rows = CAP * PER
    for n in range(CHUNKS):
        if n:
            loop(n * PER // GROUP, (n + 1) * PER // GROUP, token_step)
        landed(tr.at[1 - core, n], tf_recv.at[n])

        def unpack(b):
            half, h = b // 2, lax.rem(b, 2)
            source = tr.at[half, n, pl.ds(h, 2)].reshape(2 * 8 * PER, COLS)
            for c in range(COLS // STEP):
                cols = slice(c * STEP, (c + 1) * STEP)
                xd[b, :, cols] = dot(perm_in[h], source[:, cols]).astype(BF)

        loop(0, 4, unpack)
        pre[...] = jnp.zeros_like(pre)

        def project(b):
            gate_up = wr.at[b, pl.ds(0, 2)].reshape(2 * NE * 8, COLS)
            down = wr.at[b, 2].reshape(NE * 8, COLS)
            pre[:, : 2 * NE * 8] += dot_t(xd[b, :rows], gate_up[...])
            pre[:, 2 * NE * 8 :] += dot_t(xd[b, rows:], down[...])

        loop(0, 4, project)
        width = NE * 8
        gate, up, back = pre[:, :width], pre[:, width : 2 * width], pre[:, 2 * width :]
        s = jax.nn.sigmoid(gate)
        hidden = (gate * s * up).astype(BF)
        grad_gate = (back * up * s * (1.0 + gate * (1.0 - s))).astype(BF)
        grad_up = (back * gate * s).astype(BF)
        grads = jnp.concatenate([grad_gate, grad_up], axis=1)

        def part(b, put):
            gate_up = wr.at[b, pl.ds(0, 2)].reshape(2 * NE * 8, COLS)
            down = wr.at[b, 2].reshape(NE * 8, COLS)
            for c in range(COLS // STEP):
                cols = slice(c * STEP, (c + 1) * STEP)
                put(slice(0, rows), cols, dot(hidden, down[:, cols]))
                put(slice(rows, 2 * rows), cols, dot(grads, gate_up[:, cols]))

        def part_copy(h):
            return pltpu.make_async_remote_copy(
                src_ref=ps.at[n, h],
                dst_ref=pr.at[n, h],
                send_sem=p_send.at[n, h],
                recv_sem=p_recv.at[n, h],
                device_id=partner,
                device_id_type=MESH,
            )

        for h in range(2):

            def put_sent(at, cols, value):
                ps[n, h, at, cols] = value.astype(BF)

            part((1 - core) * 2 + h, put_sent)
            part_copy(h).start()
        for h in range(2):

            def put_own(at, cols, value):
                own[h, at, cols] = value.astype(BF)

            part(core * 2 + h, put_own)
        for h in range(2):
            part_copy(h).wait_recv()
            ob[h * 2 * rows : (h + 1) * 2 * rows, :] = (
                own[h].astype(F32) + pr[n, h].astype(F32)
            ).astype(BF)
        for t in range(TILES):
            for c in range(COLS // STEP):
                cols = slice(c * STEP, (c + 1) * STEP)
                moved = dot(perm_out[t], ob[t * rows : (t + 2) * rows, cols])
                rs.at[n, t].reshape(8 * PER, COLS)[:, cols] = moved.astype(BF)
        if n == 0:
            own_result.start()
            loop(1, PER, lambda i: return_copy(i).start())
        else:
            loop(n * PER, (n + 1) * PER, lambda i: return_copy(i).start())

    def result_forward(g):
        group = hr.at[core, :, pl.ds(g * GROUP, GROUP)]
        return pltpu.make_async_remote_copy(
            src_ref=group,
            dst_ref=group,
            send_sem=rf_send.at[0],
            recv_sem=rf_recv.at[0],
            device_id=partner,
            device_id_type=MESH,
        )

    def result_step(g):
        landed(hr.at[core, :, pl.ds(g * GROUP, GROUP)], r_recv.at[g])
        result_forward(g).start()

    own_result.wait()
    landed(hr.at[core, :, pl.ds(1, GROUP - 1)], r_recv.at[0])
    result_forward(0).start()
    loop(1, GROUPS, result_step)

    left(ws.at[:, pl.ds(0, NE - 1)], w_send.at[0])
    left(ts.at[:, pl.ds(0, NE - 1)], t_send.at[0])
    left(hr.at[core, :, pl.ds(0, NE - 1)], r_send.at[0])
    left(wr.at[pl.ds(0, 3)], y_send.at[0])
    left(tr.at[core], tf_send.at[0])
    for n in range(CHUNKS):
        for h in range(2):
            left(ps.at[n, h], p_send.at[n, h])
    left(hr.at[core], rf_send.at[0])
    landed(hr.at[1 - core], rf_recv.at[0])


def finish(hr, table, out_ref, grad_ref):
    b = pl.program_id(0)
    half, h = b // 2, lax.rem(b, 2)
    n_tok = out_ref.shape[0]
    source = hr.at[half, pl.ds(h, 2)].reshape(2 * NE * 8, COLS)
    for c in range(COLS // STEP):
        cols = slice(c * STEP, (c + 1) * STEP)
        value = dot(table[h], source[:, cols]).astype(BF)
        out_ref[:, cols] = value[:n_tok]
        grad_ref[:, cols] = value[n_tok:]


def per_device(tokens, cotangent, routes, cluster, w_gate, w_up, w_down):
    n_tok, width = tokens.shape
    rows_dev = w_gate.shape[0]
    dma = pltpu.SemaphoreType.DMA
    rows = CAP * PER
    vmem = pl.BlockSpec(memory_space=pltpu.VMEM)
    results, table = pl.pallas_call(
        kernel,
        out_shape=(
            pltpu.VMEM((2, TILES, NE, 8, COLS), BF),
            pltpu.VMEM((2, 2 * n_tok, 2 * NE * 8), BF),
        ),
        in_specs=[pl.BlockSpec(memory_space=pltpu.HBM)] * 7,
        out_specs=(vmem, vmem),
        scratch_shapes=[
            pltpu.VMEM((n_tok, width), BF),
            pltpu.VMEM((n_tok, width), BF),
            pltpu.VMEM((1, n_tok), jnp.int32),
            pltpu.VMEM(cluster.shape, jnp.int32),
            pltpu.VMEM((3, rows_dev, w_gate.shape[1]), BF),
            pltpu.VMEM((NE * 8, rows_dev), F32),
            pltpu.VMEM((3, NE, 8, COLS), BF),
            pltpu.VMEM((NDP, 3, NE, 8, COLS), BF),
            pltpu.VMEM((TILES, NE, 8, COLS), BF),
            pltpu.VMEM((2, CHUNKS, TILES, PER, 8, COLS), BF),
            pltpu.VMEM((4, 2 * rows, COLS), BF),
            pltpu.VMEM((rows, 3 * NE * 8), F32),
            pltpu.VMEM((CHUNKS, 2, 2 * rows, COLS), BF),
            pltpu.VMEM((CHUNKS, 2, 2 * rows, COLS), BF),
            pltpu.VMEM((2, 2 * rows, COLS), BF),
            pltpu.VMEM((4 * rows, COLS), BF),
            pltpu.VMEM((CHUNKS, TILES, PER, 8, COLS), BF),
            pltpu.VMEM((2, 2 * rows, 2 * 8 * PER), BF),
            pltpu.VMEM((TILES, 8 * PER, 2 * rows), BF),
            dma((7,)),
            dma((4,)),
            dma((1,)),
            dma((GROUPS,)),
            dma((1,)),
            dma((3, GROUPS)),
            dma((1,)),
            dma((GROUPS,)),
            dma((1,)),
            dma((CHUNKS,)),
            dma((CHUNKS, 2)),
            dma((CHUNKS, 2)),
            dma((1,)),
            dma((GROUPS,)),
            dma((1,)),
            dma((1,)),
        ],
        compiler_params=pltpu.CompilerParams(
            collective_id=0, has_side_effects=True, vmem_limit_bytes=VMEM_BYTES
        ),
    )(tokens, cotangent, routes.reshape(1, n_tok), cluster, w_gate, w_up, w_down)
    column = pl.BlockSpec((n_tok, COLS), lambda b: (0, b))
    shape = jax.ShapeDtypeStruct((n_tok, width), BF)
    return pl.pallas_call(
        finish,
        grid=(width // COLS,),
        out_shape=(shape, shape),
        in_specs=[vmem, vmem],
        out_specs=(column, column),
        compiler_params=pltpu.CompilerParams(vmem_limit_bytes=16 << 20),
    )(results, table)


def solution(mesh):
    in_specs = (
        P(("dp", "expert"), None),
        P(("dp", "expert"), None),
        P(("dp", "expert"), None),
        P(),
        P(("expert", "tensor"), "dp"),
        P(("expert", "tensor"), "dp"),
        P(("expert", "tensor"), "dp"),
    )
    out_specs = (P(("dp", "expert"), None), P(("dp", "expert"), None))
    return jax.shard_map(
        per_device, mesh=mesh, in_specs=in_specs, out_specs=out_specs, check_vma=False
    )
```

```python
import functools

import jax
import jax.numpy as jnp
from jax import lax
from jax.experimental import pallas as pl
from jax.experimental.pallas import tpu as pltpu
from jax.sharding import PartitionSpec as P

NX, NZ = 4, 8
NE = NX * NZ
NDP = 4
CAP = 6
TILES = 3
CHUNKS = 2
PER = NE // CHUNKS
COLS = 1024
STEP = 512
GROUP = 4
GROUPS = NE // GROUP
LAST = NE - GROUP
STEPS = [(dx, dz) for dz in (0, 1, 7, 2, 6, 3, 5, 4) for dx in range(NX)]
HOME = STEPS.index((0, 0))
MESH = pl.DeviceIdType.MESH
VMEM_BYTES = 67_043_328 - (2 * TILES * NE * 8 * COLS + 4 * 256 * 256 + 4 * 256 * COLS) * 2
BF = jnp.bfloat16
F32 = jnp.float32


def iota(shape, dim):
    return lax.broadcasted_iota(jnp.int32, shape, dim)


def onehot(mask):
    return jnp.where(mask, 1.0, 0.0).astype(BF)


def dot(a, b):
    return jnp.dot(a, b, preferred_element_type=F32)


def dot_t(a, b):
    return lax.dot_general(a, b, (((1,), (1,)), ((), ())), preferred_element_type=F32)


def along_z(k):
    odd, half = lax.rem(k, 2), (k + 1) // 2
    return lax.rem(odd * half + (1 - odd) * (NZ - half), NZ)


def by_x(i):
    j = i // NZ
    return lax.rem(j, 2) * 2 + j // 2, along_z(lax.rem(i, NZ))


def kernel(
    tok_hbm,
    cot_hbm,
    routes_hbm,
    cluster_hbm,
    wg_hbm,
    wu_hbm,
    wd_hbm,
    hr,
    table,
    part_out,
    tok_ref,
    cot_ref,
    routes_ref,
    cluster_ref,
    w_ref,
    sel,
    ws,
    wr,
    ts,
    tr,
    xd,
    pre,
    ps,
    pr,
    own,
    ob,
    rs,
    perm_in,
    perm_out,
    in_sem,
    local_sem,
    w_send,
    w_recv,
    y_send,
    y_recv,
    t_send,
    t_recv,
    tf_send,
    tf_recv,
    p_send,
    p_recv,
    r_send,
    r_recv,
    rf_send,
    rf_recv,
):
    dp = lax.axis_index("dp")
    me = lax.axis_index("expert")
    core = lax.axis_index("tensor")
    mx, mz = me // NZ, lax.rem(me, NZ)
    shard = me * 2 + core
    rows_dev = w_ref.shape[1]
    n_tok = tok_ref.shape[0]
    partner = (dp, me, 1 - core)

    def ahead(step):
        return lax.rem(mx + step[0], NX) * NZ + lax.rem(mz + step[1], NZ)

    def behind(step):
        return lax.rem(mx + NX - step[0], NX) * NZ + lax.rem(mz + NZ - step[1], NZ)

    def plane(step):
        return lax.rem(dp + NDP + step, NDP)

    def loop(lower, upper, body):
        def run(i, carry):
            body(i)
            return carry

        lax.fori_loop(lower, upper, run, 0)

    pulls = [
        pltpu.make_async_copy(source, target, in_sem.at[k])
        for k, (source, target) in enumerate(
            (
                (cluster_hbm, cluster_ref),
                (wg_hbm, w_ref.at[0]),
                (wu_hbm, w_ref.at[1]),
                (wd_hbm, w_ref.at[2]),
                (routes_hbm, routes_ref),
                (tok_hbm, tok_ref),
                (cot_hbm, cot_ref),
            )
        )
    ]
    for pull in pulls[:4]:
        pull.start()

    barrier = pltpu.get_barrier_semaphore()
    for step in reversed(STEPS):
        if step != (0, 0):
            pl.semaphore_signal(barrier, 1, device_id=(dp, ahead(step), core), device_id_type=MESH)
    pl.semaphore_signal(barrier, 1, device_id=(plane(1), me, core), device_id_type=MESH)
    pl.semaphore_signal(barrier, 1, device_id=(plane(-1), me, core), device_id_type=MESH)
    pl.semaphore_signal(barrier, 1, device_id=partner, device_id_type=MESH)
    for pull in pulls[4:]:
        pull.start()

    def weight_copy(i):
        return pltpu.make_async_remote_copy(
            src_ref=ws.at[:, i],
            dst_ref=wr.at[dp, :, i],
            send_sem=w_send.at[0],
            recv_sem=w_recv.at[i // GROUP],
            device_id=(dp, ahead(STEPS[i]), core),
            device_id_type=MESH,
        )

    half_slots = cluster_ref.shape[1] // 2
    sub = iota((8, 1), 0)
    slot = (sub // 4) * half_slots + shard * 4 + lax.rem(sub, 4)
    lanes = iota((8, cluster_ref.shape[1]), 1)
    neuron = iota((8, rows_dev), 1) + shard * rows_dev
    own_weights = pltpu.make_async_copy(ws.at[:, HOME], wr.at[dp, :, HOME], local_sem.at[0])
    pulls[0].wait()
    for g in range(GROUPS):
        pieces = range(g * GROUP, (g + 1) * GROUP)
        for i in pieces:
            line = jnp.broadcast_to(cluster_ref[pl.ds(ahead(STEPS[i]), 1), :], lanes.shape)
            pick = jnp.sum(jnp.where(lanes == slot, line, 0), axis=1, keepdims=True)
            sel[i * 8 : i * 8 + 8, :] = jnp.where(neuron == pick, 1.0, 0.0)
        chosen = sel[g * GROUP * 8 : (g + 1) * GROUP * 8, :].astype(BF)
        for a in range(3):
            if g == 0:
                pulls[1 + a].wait()
            picked = ws.at[a, g * GROUP : (g + 1) * GROUP].reshape(GROUP * 8, COLS)
            picked[...] = dot(chosen, w_ref[a]).astype(BF)
        if g == 1:
            pl.semaphore_wait(barrier, NE - 1 + 3)
        if g == 0:
            continue
        for i in range(g * GROUP if g > 1 else 0, (g + 1) * GROUP):
            if i == HOME:
                own_weights.start()
            else:
                weight_copy(i).start()

    def landed(ref, sem):
        pltpu.make_async_remote_copy(
            src_ref=ref,
            dst_ref=ref,
            send_sem=local_sem.at[3],
            recv_sem=sem,
            device_id=partner,
            device_id_type=MESH,
        ).wait_recv()

    def left(ref, sem):
        pltpu.make_async_remote_copy(
            src_ref=ref,
            dst_ref=ref,
            send_sem=sem,
            recv_sem=local_sem.at[3],
            device_id=partner,
            device_id_type=MESH,
        ).wait_send()

    for pull in pulls[4:]:
        pull.wait()

    square = (n_tok, n_tok)
    by_lane = jnp.broadcast_to(routes_ref[...], square)
    eye = iota(square, 0) == iota(square, 1)
    route_col = jnp.sum(jnp.where(eye, by_lane, 0), axis=1, keepdims=True)
    same = by_lane == route_col
    place_row = jnp.sum(
        jnp.where(same & (iota(square, 0) < iota(square, 1)), 1, 0), axis=0, keepdims=True
    )
    place_col = jnp.sum(
        jnp.where(same & (iota(square, 1) < iota(square, 0)), 1, 0), axis=1, keepdims=True
    )
    route_row = routes_ref[...]

    tall = (NE * 8, n_tok)
    row = iota(tall, 0)
    row_expert, row_sub = row // 8, lax.rem(row, 8)
    mine = row_expert == route_row
    for t in range(TILES):
        lhs = [onehot(mine & (place_row == row_sub + 8 * t - CAP * (t + j))) for j in range(2)]
        for c in range(COLS // STEP):
            total = None
            for j in range(2):
                block, source = (t + j) // 2, (tok_ref, cot_ref)[(t + j) % 2]
                first = pl.multiple_of(core * 2 * COLS + block * COLS + c * STEP, STEP)
                term = dot(lhs[j], source[:, pl.ds(first, STEP)])
                total = term if total is None else total + term
            ts.at[t].reshape(NE * 8, COLS)[:, c * STEP : (c + 1) * STEP] = total.astype(BF)

    def token_copy(i):
        to = ahead(by_x(i))
        return pltpu.make_async_remote_copy(
            src_ref=ts.at[:, to],
            dst_ref=tr.at[core, i // PER, :, lax.rem(i, PER)],
            send_sem=t_send.at[0],
            recv_sem=t_recv.at[i // GROUP],
            device_id=(dp, to, core),
            device_id_type=MESH,
        )

    own_tokens = pltpu.make_async_copy(ts.at[:, me], tr.at[core, 0, :, 0], local_sem.at[1])
    own_tokens.start()
    loop(1, NE, lambda i: token_copy(i).start())

    long = (n_tok, 2 * 8 * PER)
    q = iota(long, 1)
    j = jnp.where(q >= 8 * PER, 1, 0)
    q = q - j * (8 * PER)
    for n in range(CHUNKS):
        here = route_col == ahead(by_x(q // 8 + n * PER))
        for h in range(2):
            for b in range(2):
                spot = place_col == lax.rem(q, 8) + 8 * (h + j) - CAP * (2 * h + b)
                table[n, h, b * n_tok : (b + 1) * n_tok, :] = onehot(here & spot)

    wide = (2 * CAP * PER, 2 * 8 * PER)
    r, q = iota(wide, 0), iota(wide, 1)
    a = jnp.where(r >= CAP * PER, 1, 0)
    t = jnp.where(q >= 8 * PER, 1, 0)
    r = r - a * (CAP * PER)
    q = q - t * (8 * PER)
    for h in range(2):
        p = lax.rem(q, 8) + 8 * (t + h) - CAP * (2 * h + a)
        perm_in[h] = onehot((p >= 0) & (p < CAP) & (r == CAP * (q // 8) + p))
    wide = (8 * PER, 2 * CAP * PER)
    r, q = iota(wide, 0), iota(wide, 1)
    j = jnp.where(q >= CAP * PER, 1, 0)
    q = q - j * (CAP * PER)
    for t in range(TILES):
        p = 2 * t + lax.rem(r, 8) - CAP * j
        perm_out[t] = onehot((p >= 0) & (p < CAP) & (q == CAP * (r // 8) + p))

    def plane_copy(g, which, step, way):
        group = wr.at[which, :, pl.ds(g * GROUP, GROUP)]
        return pltpu.make_async_remote_copy(
            src_ref=group,
            dst_ref=group,
            send_sem=y_send.at[0],
            recv_sem=y_recv.at[way, g],
            device_id=(plane(step), me, core),
            device_id_type=MESH,
        )

    def relay_copy(g):
        sign = 1 - 2 * lax.rem(g, 2)
        return plane_copy(g, plane(-sign), sign, 2)

    def spread(g):
        plane_copy(g, dp, 1, 0).start()
        plane_copy(g, dp, -1, 1).start()

    def relay(g):
        plane_copy(g, plane(-1), 1, 0).wait_recv()
        plane_copy(g, plane(1), -1, 1).wait_recv()
        relay_copy(g).start()

    for g in range(GROUPS):
        if g == HOME // GROUP:
            own_weights.wait()
            landed(wr.at[dp, :, pl.ds(g * GROUP + 1, GROUP - 1)], w_recv.at[g])
        else:
            landed(wr.at[dp, :, pl.ds(g * GROUP, GROUP)], w_recv.at[g])
        spread(g)
        if g:
            relay(g - 1)
    relay(GROUPS - 1)

    def token_group(g):
        per = PER // GROUP
        return tr.at[core, g // per, :, pl.ds(lax.rem(g, per) * GROUP, GROUP)]

    def token_forward(g):
        return pltpu.make_async_remote_copy(
            src_ref=token_group(g),
            dst_ref=token_group(g),
            send_sem=tf_send.at[0],
            recv_sem=tf_recv.at[g // (PER // GROUP)],
            device_id=partner,
            device_id_type=MESH,
        )

    def token_step(g):
        landed(token_group(g), t_recv.at[g])
        token_forward(g).start()

    own_tokens.wait()
    landed(tr.at[core, 0, :, pl.ds(1, GROUP - 1)], t_recv.at[0])
    token_forward(0).start()
    loop(1, PER // GROUP, token_step)

    def return_copy(i):
        return pltpu.make_async_remote_copy(
            src_ref=rs.at[i // PER, :, lax.rem(i, PER)],
            dst_ref=hr.at[core, i // PER, :, lax.rem(i, PER)],
            send_sem=r_send.at[0],
            recv_sem=r_recv.at[i // GROUP + (i // LAST) * (i - LAST)],
            device_id=(dp, behind(by_x(i)), core),
            device_id_type=MESH,
        )

    own_result = pltpu.make_async_copy(rs.at[0, :, 0], hr.at[core, 0, :, 0], local_sem.at[2])
    rows = CAP * PER
    for n in range(CHUNKS):
        if n:
            loop(n * PER // GROUP, (n + 1) * PER // GROUP, token_step)
        landed(tr.at[1 - core, n], tf_recv.at[n])

        def unpack(b):
            half, h = b // 2, lax.rem(b, 2)
            source = tr.at[half, n, pl.ds(h, 2)].reshape(2 * 8 * PER, COLS)
            for c in range(COLS // STEP):
                cols = slice(c * STEP, (c + 1) * STEP)
                xd[b, :, cols] = dot(perm_in[h], source[:, cols]).astype(BF)

        loop(0, 4, unpack)
        pre[...] = jnp.zeros_like(pre)

        def project(b):
            gate_up = wr.at[b, pl.ds(0, 2)].reshape(2 * NE * 8, COLS)
            down = wr.at[b, 2].reshape(NE * 8, COLS)
            pre[:, : 2 * NE * 8] += dot_t(xd[b, :rows], gate_up[...])
            pre[:, 2 * NE * 8 :] += dot_t(xd[b, rows:], down[...])

        project(dp)
        project(plane(1))
        project(plane(-1))
        if n == 0:
            loop(0, GROUPS, lambda g: relay_copy(g).wait_recv())
        project(plane(2))
        width = NE * 8
        gate, up, back = pre[:, :width], pre[:, width : 2 * width], pre[:, 2 * width :]
        s = jax.nn.sigmoid(gate)
        hidden = (gate * s * up).astype(BF)
        grad_gate = (back * up * s * (1.0 + gate * (1.0 - s))).astype(BF)
        grad_up = (back * gate * s).astype(BF)
        grads = jnp.concatenate([grad_gate, grad_up], axis=1)

        def part(b, put):
            gate_up = wr.at[b, pl.ds(0, 2)].reshape(2 * NE * 8, COLS)
            down = wr.at[b, 2].reshape(NE * 8, COLS)
            for c in range(COLS // STEP):
                cols = slice(c * STEP, (c + 1) * STEP)
                put(slice(0, rows), cols, dot(hidden, down[:, cols]))
                put(slice(rows, 2 * rows), cols, dot(grads, gate_up[:, cols]))

        def part_copy(h):
            return pltpu.make_async_remote_copy(
                src_ref=ps.at[n, h],
                dst_ref=pr.at[n, h],
                send_sem=p_send.at[n, h],
                recv_sem=p_recv.at[n, h],
                device_id=partner,
                device_id_type=MESH,
            )

        for h in range(2):

            def put_sent(at, cols, value):
                ps[n, h, at, cols] = value.astype(BF)

            part((1 - core) * 2 + h, put_sent)
            part_copy(h).start()
        for h in range(2):

            def put_own(at, cols, value):
                own[h, at, cols] = value.astype(BF)

            part(core * 2 + h, put_own)
        for h in range(2):
            part_copy(h).wait_recv()
            ob[h * 2 * rows : (h + 1) * 2 * rows, :] = (
                own[h].astype(F32) + pr[n, h].astype(F32)
            ).astype(BF)
        for t in range(TILES):
            for c in range(COLS // STEP):
                cols = slice(c * STEP, (c + 1) * STEP)
                moved = dot(perm_out[t], ob[t * rows : (t + 2) * rows, cols])
                rs.at[n, t].reshape(8 * PER, COLS)[:, cols] = moved.astype(BF)
        if n == 0:
            own_result.start()
            left(ws.at[:, pl.ds(0, NE - 1)], t_send.at[0])
            loop(1, PER, lambda i: return_copy(i).start())
        else:
            loop(n * PER, (n + 1) * PER, lambda i: return_copy(i).start())

    def result_group(g, count):
        per = PER // GROUP
        return hr.at[core, g // per, :, pl.ds(lax.rem(g, per) * GROUP, count)]

    def result_forward(group, n):
        return pltpu.make_async_remote_copy(
            src_ref=group,
            dst_ref=group,
            send_sem=rf_send.at[0],
            recv_sem=rf_recv.at[n],
            device_id=partner,
            device_id_type=MESH,
        )

    def result_step(g):
        group = result_group(g, GROUP)
        landed(group, r_recv.at[g])
        result_forward(group, g // (PER // GROUP)).start()

    own_result.wait()
    landed(hr.at[core, 0, :, pl.ds(1, GROUP - 1)], r_recv.at[0])
    result_forward(result_group(0, GROUP), 0).start()
    loop(1, PER // GROUP, result_step)
    landed(hr.at[1 - core, 0], rf_recv.at[0])

    def settle(b):
        half, h = b // 2, lax.rem(b, 2)
        source = hr.at[half, 0, pl.ds(h, 2)].reshape(2 * 8 * PER, COLS)
        for c in range(COLS // STEP):
            cols = slice(c * STEP, (c + 1) * STEP)
            part_out[b, :, cols] = dot(table[0, h], source[:, cols]).astype(BF)

    loop(0, 4, settle)
    loop(PER // GROUP, GROUPS - 1, result_step)
    for i in range(GROUP):
        piece = hr.at[core, CHUNKS - 1, :, pl.ds(PER - GROUP + i, 1)]
        landed(piece, r_recv.at[GROUPS - 1 + i])
        result_forward(piece, CHUNKS - 1).start()

    left(ws.at[:, pl.ds(0, NE - 1)], w_send.at[0])
    left(ws.at[:, pl.ds(0, NE - 1)], r_send.at[0])
    left(wr.at[pl.ds(0, 3)], y_send.at[0])
    left(tr.at[core], tf_send.at[0])
    for n in range(CHUNKS):
        for h in range(2):
            left(ps.at[n, h], p_send.at[n, h])
    left(hr.at[core], rf_send.at[0])
    landed(hr.at[1 - core, CHUNKS - 1], rf_recv.at[CHUNKS - 1])


def finish(hr, table, part_out, out_ref, grad_ref):
    b = pl.program_id(0)
    half, h = b // 2, lax.rem(b, 2)
    n_tok = out_ref.shape[0]
    last = CHUNKS - 1
    source = hr.at[half, last, pl.ds(h, 2)].reshape(2 * 8 * PER, COLS)
    for c in range(COLS // STEP):
        cols = slice(c * STEP, (c + 1) * STEP)
        value = (dot(table[last, h], source[:, cols]) + part_out[b, :, cols].astype(F32)).astype(BF)
        out_ref[:, cols] = value[:n_tok]
        grad_ref[:, cols] = value[n_tok:]


def per_device(tokens, cotangent, routes, cluster, w_gate, w_up, w_down):
    n_tok, width = tokens.shape
    rows_dev = w_gate.shape[0]
    dma = pltpu.SemaphoreType.DMA
    rows = CAP * PER
    vmem = pl.BlockSpec(memory_space=pltpu.VMEM)
    results, table, settled = pl.pallas_call(
        kernel,
        out_shape=(
            pltpu.VMEM((2, CHUNKS, TILES, PER, 8, COLS), BF),
            pltpu.VMEM((CHUNKS, 2, 2 * n_tok, 2 * 8 * PER), BF),
            pltpu.VMEM((4, 2 * n_tok, COLS), BF),
        ),
        in_specs=[pl.BlockSpec(memory_space=pltpu.HBM)] * 7,
        out_specs=(vmem, vmem, vmem),
        scratch_shapes=[
            pltpu.VMEM((n_tok, width), BF),
            pltpu.VMEM((n_tok, width), BF),
            pltpu.VMEM((1, n_tok), jnp.int32),
            pltpu.VMEM(cluster.shape, jnp.int32),
            pltpu.VMEM((3, rows_dev, w_gate.shape[1]), BF),
            pltpu.VMEM((NE * 8, rows_dev), F32),
            pltpu.VMEM((3, NE, 8, COLS), BF),
            pltpu.VMEM((NDP, 3, NE, 8, COLS), BF),
            pltpu.VMEM((TILES, NE, 8, COLS), BF),
            pltpu.VMEM((2, CHUNKS, TILES, PER, 8, COLS), BF),
            pltpu.VMEM((4, 2 * rows, COLS), BF),
            pltpu.VMEM((rows, 3 * NE * 8), F32),
            pltpu.VMEM((CHUNKS, 2, 2 * rows, COLS), BF),
            pltpu.VMEM((CHUNKS, 2, 2 * rows, COLS), BF),
            pltpu.VMEM((2, 2 * rows, COLS), BF),
            pltpu.VMEM((4 * rows, COLS), BF),
            pltpu.VMEM((CHUNKS, TILES, PER, 8, COLS), BF),
            pltpu.VMEM((2, 2 * rows, 2 * 8 * PER), BF),
            pltpu.VMEM((TILES, 8 * PER, 2 * rows), BF),
            dma((7,)),
            dma((4,)),
            dma((1,)),
            dma((GROUPS,)),
            dma((1,)),
            dma((3, GROUPS)),
            dma((1,)),
            dma((GROUPS,)),
            dma((1,)),
            dma((CHUNKS,)),
            dma((CHUNKS, 2)),
            dma((CHUNKS, 2)),
            dma((1,)),
            dma((GROUPS - 1 + GROUP,)),
            dma((1,)),
            dma((CHUNKS,)),
        ],
        compiler_params=pltpu.CompilerParams(
            collective_id=0, has_side_effects=True, vmem_limit_bytes=VMEM_BYTES
        ),
    )(tokens, cotangent, routes.reshape(1, n_tok), cluster, w_gate, w_up, w_down)
    column = pl.BlockSpec((n_tok, COLS), lambda b: (0, b))
    shape = jax.ShapeDtypeStruct((n_tok, width), BF)
    return pl.pallas_call(
        finish,
        grid=(width // COLS,),
        out_shape=(shape, shape),
        in_specs=[vmem, vmem, vmem],
        out_specs=(column, column),
        compiler_params=pltpu.CompilerParams(vmem_limit_bytes=16 << 20),
    )(results, table, settled)


def solution(mesh):
    in_specs = (
        P(("dp", "expert"), None),
        P(("dp", "expert"), None),
        P(("dp", "expert"), None),
        P(),
        P(("expert", "tensor"), "dp"),
        P(("expert", "tensor"), "dp"),
        P(("expert", "tensor"), "dp"),
    )
    out_specs = (P(("dp", "expert"), None), P(("dp", "expert"), None))
    return jax.shard_map(
        per_device, mesh=mesh, in_specs=in_specs, out_specs=out_specs, check_vma=False
    )
```

```python
import functools

import jax
import jax.numpy as jnp
from jax import lax
from jax.experimental import pallas as pl
from jax.experimental.pallas import tpu as pltpu
from jax.sharding import PartitionSpec as P

NX, NZ = 4, 8
NE = NX * NZ
NDP = 4
CAP = 6
TILES = 3
CHUNKS = 2
PER = NE // CHUNKS
COLS = 1024
STEP = 512
GROUP = 4
GROUPS = NE // GROUP
LAST = NE - GROUP
STEPS = [(dx, dz) for dz in (0, 1, 7, 2, 6, 3, 5, 4) for dx in range(NX)]
HOME = STEPS.index((0, 0))
MESH = pl.DeviceIdType.MESH
VMEM_BYTES = 67_043_328 - (2 * TILES * NE * 8 * COLS + 4 * 256 * 256 + 4 * 256 * COLS) * 2
BF = jnp.bfloat16
F32 = jnp.float32


def iota(shape, dim):
    return lax.broadcasted_iota(jnp.int32, shape, dim)


def onehot(mask):
    return jnp.where(mask, 1.0, 0.0).astype(BF)


def dot(a, b):
    return jnp.dot(a, b, preferred_element_type=F32)


def dot_t(a, b):
    return lax.dot_general(a, b, (((1,), (1,)), ((), ())), preferred_element_type=F32)


def along_z(k):
    odd, half = lax.rem(k, 2), (k + 1) // 2
    return lax.rem(odd * half + (1 - odd) * (NZ - half), NZ)


def by_x(i):
    j = i // NZ
    return lax.rem(j, 2) * 2 + j // 2, along_z(lax.rem(i, NZ))


def kernel(
    tok_hbm,
    cot_hbm,
    routes_hbm,
    cluster_hbm,
    wg_hbm,
    wu_hbm,
    wd_hbm,
    hr,
    table,
    part_out,
    tok_ref,
    cot_ref,
    routes_ref,
    cluster_ref,
    w_ref,
    sel,
    ws,
    wr,
    ts,
    tr,
    xd,
    pre,
    ps,
    pr,
    own,
    ob,
    rs,
    perm_in,
    perm_out,
    in_sem,
    local_sem,
    w_send,
    w_recv,
    y_send,
    y_recv,
    t_send,
    t_recv,
    tf_send,
    tf_recv,
    p_send,
    p_recv,
    r_send,
    r_recv,
    rf_send,
    rf_recv,
):
    dp = lax.axis_index("dp")
    me = lax.axis_index("expert")
    core = lax.axis_index("tensor")
    mx, mz = me // NZ, lax.rem(me, NZ)
    shard = me * 2 + core
    rows_dev = w_ref.shape[1]
    n_tok = tok_ref.shape[0]
    partner = (dp, me, 1 - core)

    def ahead(step):
        return lax.rem(mx + step[0], NX) * NZ + lax.rem(mz + step[1], NZ)

    def behind(step):
        return lax.rem(mx + NX - step[0], NX) * NZ + lax.rem(mz + NZ - step[1], NZ)

    def plane(step):
        return lax.rem(dp + NDP + step, NDP)

    def loop(lower, upper, body):
        def run(i, carry):
            body(i)
            return carry

        lax.fori_loop(lower, upper, run, 0)

    pulls = [
        pltpu.make_async_copy(source, target, in_sem.at[k])
        for k, (source, target) in enumerate(
            (
                (cluster_hbm, cluster_ref),
                (wg_hbm, w_ref.at[0]),
                (wu_hbm, w_ref.at[1]),
                (wd_hbm, w_ref.at[2]),
                (routes_hbm, routes_ref),
                (tok_hbm, tok_ref),
                (cot_hbm, cot_ref),
            )
        )
    ]
    for pull in pulls[:4]:
        pull.start()

    barrier = pltpu.get_barrier_semaphore()
    for step in reversed(STEPS):
        if step != (0, 0):
            pl.semaphore_signal(barrier, 1, device_id=(dp, ahead(step), core), device_id_type=MESH)
    pl.semaphore_signal(barrier, 1, device_id=(plane(1), me, core), device_id_type=MESH)
    pl.semaphore_signal(barrier, 1, device_id=(plane(-1), me, core), device_id_type=MESH)
    pl.semaphore_signal(barrier, 1, device_id=partner, device_id_type=MESH)
    for pull in pulls[4:]:
        pull.start()

    def weight_copy(i):
        return pltpu.make_async_remote_copy(
            src_ref=ws.at[:, i],
            dst_ref=wr.at[dp, :, i],
            send_sem=w_send.at[0],
            recv_sem=w_recv.at[i // GROUP],
            device_id=(dp, ahead(STEPS[i]), core),
            device_id_type=MESH,
        )

    half_slots = cluster_ref.shape[1] // 2
    sub = iota((8, 1), 0)
    slot = (sub // 4) * half_slots + shard * 4 + lax.rem(sub, 4)
    lanes = iota((8, cluster_ref.shape[1]), 1)
    neuron = iota((8, rows_dev), 1) + shard * rows_dev
    own_weights = pltpu.make_async_copy(ws.at[:, HOME], wr.at[dp, :, HOME], local_sem.at[0])
    pulls[0].wait()
    for g in range(GROUPS):
        pieces = range(g * GROUP, (g + 1) * GROUP)
        for i in pieces:
            line = jnp.broadcast_to(cluster_ref[pl.ds(ahead(STEPS[i]), 1), :], lanes.shape)
            pick = jnp.sum(jnp.where(lanes == slot, line, 0), axis=1, keepdims=True)
            sel[i * 8 : i * 8 + 8, :] = jnp.where(neuron == pick, 1.0, 0.0)
        chosen = sel[g * GROUP * 8 : (g + 1) * GROUP * 8, :].astype(BF)
        for a in range(3):
            if g == 0:
                pulls[1 + a].wait()
            picked = ws.at[a, g * GROUP : (g + 1) * GROUP].reshape(GROUP * 8, COLS)
            picked[...] = dot(chosen, w_ref[a]).astype(BF)
        if g == 1:
            pl.semaphore_wait(barrier, NE - 1 + 3)
        if g == 0:
            continue
        for i in range(g * GROUP if g > 1 else 0, (g + 1) * GROUP):
            if i == HOME:
                own_weights.start()
            else:
                weight_copy(i).start()

    def landed(ref, sem):
        pltpu.make_async_remote_copy(
            src_ref=ref,
            dst_ref=ref,
            send_sem=local_sem.at[3],
            recv_sem=sem,
            device_id=partner,
            device_id_type=MESH,
        ).wait_recv()

    def left(ref, sem):
        pltpu.make_async_remote_copy(
            src_ref=ref,
            dst_ref=ref,
            send_sem=sem,
            recv_sem=local_sem.at[3],
            device_id=partner,
            device_id_type=MESH,
        ).wait_send()

    for pull in pulls[4:]:
        pull.wait()

    square = (n_tok, n_tok)
    by_lane = jnp.broadcast_to(routes_ref[...], square)
    eye = iota(square, 0) == iota(square, 1)
    route_col = jnp.sum(jnp.where(eye, by_lane, 0), axis=1, keepdims=True)
    same = by_lane == route_col
    place_row = jnp.sum(
        jnp.where(same & (iota(square, 0) < iota(square, 1)), 1, 0), axis=0, keepdims=True
    )
    place_col = jnp.sum(
        jnp.where(same & (iota(square, 1) < iota(square, 0)), 1, 0), axis=1, keepdims=True
    )
    route_row = routes_ref[...]

    tall = (NE * 8, n_tok)
    row = iota(tall, 0)
    row_expert, row_sub = row // 8, lax.rem(row, 8)
    mine = row_expert == route_row
    for t in range(TILES):
        lhs = [onehot(mine & (place_row == row_sub + 8 * t - CAP * (t + j))) for j in range(2)]
        for c in range(COLS // STEP):
            total = None
            for j in range(2):
                block, source = (t + j) // 2, (tok_ref, cot_ref)[(t + j) % 2]
                first = pl.multiple_of(core * 2 * COLS + block * COLS + c * STEP, STEP)
                term = dot(lhs[j], source[:, pl.ds(first, STEP)])
                total = term if total is None else total + term
            ts.at[t].reshape(NE * 8, COLS)[:, c * STEP : (c + 1) * STEP] = total.astype(BF)

    def token_copy(i):
        to = ahead(by_x(i))
        return pltpu.make_async_remote_copy(
            src_ref=ts.at[:, to],
            dst_ref=tr.at[core, i // PER, :, lax.rem(i, PER)],
            send_sem=t_send.at[0],
            recv_sem=t_recv.at[i // GROUP],
            device_id=(dp, to, core),
            device_id_type=MESH,
        )

    own_tokens = pltpu.make_async_copy(ts.at[:, me], tr.at[core, 0, :, 0], local_sem.at[1])
    own_tokens.start()
    loop(1, NE, lambda i: token_copy(i).start())

    long = (n_tok, 2 * 8 * PER)
    q = iota(long, 1)
    j = jnp.where(q >= 8 * PER, 1, 0)
    q = q - j * (8 * PER)
    for n in range(CHUNKS):
        here = route_col == ahead(by_x(q // 8 + n * PER))
        for h in range(2):
            for b in range(2):
                spot = place_col == lax.rem(q, 8) + 8 * (h + j) - CAP * (2 * h + b)
                table[n, h, b * n_tok : (b + 1) * n_tok, :] = onehot(here & spot)

    wide = (2 * CAP * PER, 2 * 8 * PER)
    r, q = iota(wide, 0), iota(wide, 1)
    a = jnp.where(r >= CAP * PER, 1, 0)
    t = jnp.where(q >= 8 * PER, 1, 0)
    r = r - a * (CAP * PER)
    q = q - t * (8 * PER)
    for h in range(2):
        p = lax.rem(q, 8) + 8 * (t + h) - CAP * (2 * h + a)
        perm_in[h] = onehot((p >= 0) & (p < CAP) & (r == CAP * (q // 8) + p))
    wide = (8 * PER, 2 * CAP * PER)
    r, q = iota(wide, 0), iota(wide, 1)
    j = jnp.where(q >= CAP * PER, 1, 0)
    q = q - j * (CAP * PER)
    for t in range(TILES):
        p = 2 * t + lax.rem(r, 8) - CAP * j
        perm_out[t] = onehot((p >= 0) & (p < CAP) & (q == CAP * (r // 8) + p))

    def plane_copy(g, which, step, way):
        group = wr.at[which, :, pl.ds(g * GROUP, GROUP)]
        return pltpu.make_async_remote_copy(
            src_ref=group,
            dst_ref=group,
            send_sem=y_send.at[0],
            recv_sem=y_recv.at[way, g],
            device_id=(plane(step), me, core),
            device_id_type=MESH,
        )

    def relay_copy(g):
        sign = 1 - 2 * lax.rem(g, 2)
        return plane_copy(g, plane(-sign), sign, 2)

    def spread(g):
        plane_copy(g, dp, 1, 0).start()
        plane_copy(g, dp, -1, 1).start()

    def relay(g):
        plane_copy(g, plane(-1), 1, 0).wait_recv()
        plane_copy(g, plane(1), -1, 1).wait_recv()
        relay_copy(g).start()

    for g in range(GROUPS):
        if g == HOME // GROUP:
            own_weights.wait()
            landed(wr.at[dp, :, pl.ds(g * GROUP + 1, GROUP - 1)], w_recv.at[g])
        else:
            landed(wr.at[dp, :, pl.ds(g * GROUP, GROUP)], w_recv.at[g])
        spread(g)
        if g:
            relay(g - 1)
    relay(GROUPS - 1)

    def token_group(g):
        per = PER // GROUP
        return tr.at[core, g // per, :, pl.ds(lax.rem(g, per) * GROUP, GROUP)]

    def token_forward(g):
        return pltpu.make_async_remote_copy(
            src_ref=token_group(g),
            dst_ref=token_group(g),
            send_sem=tf_send.at[0],
            recv_sem=tf_recv.at[g // (PER // GROUP)],
            device_id=partner,
            device_id_type=MESH,
        )

    def token_step(g):
        landed(token_group(g), t_recv.at[g])
        token_forward(g).start()

    own_tokens.wait()
    landed(tr.at[core, 0, :, pl.ds(1, GROUP - 1)], t_recv.at[0])
    token_forward(0).start()
    loop(1, PER // GROUP, token_step)

    def return_copy(i):
        return pltpu.make_async_remote_copy(
            src_ref=rs.at[i // PER, :, lax.rem(i, PER)],
            dst_ref=hr.at[core, i // PER, :, lax.rem(i, PER)],
            send_sem=r_send.at[0],
            recv_sem=r_recv.at[i // GROUP + (i // LAST) * (i - LAST)],
            device_id=(dp, behind(by_x(i)), core),
            device_id_type=MESH,
        )

    own_result = pltpu.make_async_copy(rs.at[0, :, 0], hr.at[core, 0, :, 0], local_sem.at[2])
    rows = CAP * PER
    for n in range(CHUNKS):
        if n:
            loop(n * PER // GROUP, (n + 1) * PER // GROUP, token_step)
        landed(tr.at[1 - core, n], tf_recv.at[n])

        def unpack(b):
            half, h = b // 2, lax.rem(b, 2)
            source = tr.at[half, n, pl.ds(h, 2)].reshape(2 * 8 * PER, COLS)
            for c in range(COLS // STEP):
                cols = slice(c * STEP, (c + 1) * STEP)
                xd[b, :, cols] = dot(perm_in[h], source[:, cols]).astype(BF)

        loop(0, 4, unpack)
        pre[...] = jnp.zeros_like(pre)

        def project(b):
            gate_up = wr.at[b, pl.ds(0, 2)].reshape(2 * NE * 8, COLS)
            down = wr.at[b, 2].reshape(NE * 8, COLS)
            pre[:, : 2 * NE * 8] += dot_t(xd[b, :rows], gate_up[...])
            pre[:, 2 * NE * 8 :] += dot_t(xd[b, rows:], down[...])

        project(dp)
        project(plane(1))
        project(plane(-1))
        if n == 0:
            loop(0, GROUPS, lambda g: relay_copy(g).wait_recv())
        project(plane(2))
        width = NE * 8
        gate, up, back = pre[:, :width], pre[:, width : 2 * width], pre[:, 2 * width :]
        s = jax.nn.sigmoid(gate)
        hidden = (gate * s * up).astype(BF)
        grad_gate = (back * up * s * (1.0 + gate * (1.0 - s))).astype(BF)
        grad_up = (back * gate * s).astype(BF)
        grads = jnp.concatenate([grad_gate, grad_up], axis=1)

        def part(b, put):
            gate_up = wr.at[b, pl.ds(0, 2)].reshape(2 * NE * 8, COLS)
            down = wr.at[b, 2].reshape(NE * 8, COLS)
            for c in range(COLS // STEP):
                cols = slice(c * STEP, (c + 1) * STEP)
                put(slice(0, rows), cols, dot(hidden, down[:, cols]))
                put(slice(rows, 2 * rows), cols, dot(grads, gate_up[:, cols]))

        def part_copy(h):
            return pltpu.make_async_remote_copy(
                src_ref=ps.at[n, h],
                dst_ref=pr.at[n, h],
                send_sem=p_send.at[n, h],
                recv_sem=p_recv.at[n, h],
                device_id=partner,
                device_id_type=MESH,
            )

        for h in range(2):

            def put_sent(at, cols, value):
                ps[n, h, at, cols] = value.astype(BF)

            part((1 - core) * 2 + h, put_sent)
            part_copy(h).start()
        for h in range(2):

            def put_own(at, cols, value):
                own[h, at, cols] = value.astype(BF)

            part(core * 2 + h, put_own)
        for h in range(2):
            part_copy(h).wait_recv()
            ob[h * 2 * rows : (h + 1) * 2 * rows, :] = (
                own[h].astype(F32) + pr[n, h].astype(F32)
            ).astype(BF)
        for t in range(TILES):
            for c in range(COLS // STEP):
                cols = slice(c * STEP, (c + 1) * STEP)
                moved = dot(perm_out[t], ob[t * rows : (t + 2) * rows, cols])
                rs.at[n, t].reshape(8 * PER, COLS)[:, cols] = moved.astype(BF)
        if n == 0:
            own_result.start()
            left(ws.at[:, pl.ds(0, NE - 1)], t_send.at[0])
            loop(1, PER, lambda i: return_copy(i).start())
        else:
            loop(n * PER, (n + 1) * PER, lambda i: return_copy(i).start())

    def result_group(g, count):
        per = PER // GROUP
        return hr.at[core, g // per, :, pl.ds(lax.rem(g, per) * GROUP, count)]

    def result_forward(group, n):
        return pltpu.make_async_remote_copy(
            src_ref=group,
            dst_ref=group,
            send_sem=rf_send.at[0],
            recv_sem=rf_recv.at[n],
            device_id=partner,
            device_id_type=MESH,
        )

    def result_step(g):
        group = result_group(g, GROUP)
        landed(group, r_recv.at[g])
        result_forward(group, g // (PER // GROUP)).start()

    own_result.wait()
    landed(hr.at[core, 0, :, pl.ds(1, GROUP - 1)], r_recv.at[0])
    result_forward(result_group(0, GROUP), 0).start()
    loop(1, PER // GROUP, result_step)
    landed(hr.at[1 - core, 0], rf_recv.at[0])

    def settle(b):
        half, h = b // 2, lax.rem(b, 2)
        source = hr.at[half, 0, pl.ds(h, 2)].reshape(2 * 8 * PER, COLS)
        for c in range(COLS // STEP):
            cols = slice(c * STEP, (c + 1) * STEP)
            part_out[b, :, cols] = dot(table[0, h], source[:, cols]).astype(BF)

    loop(0, 4, settle)
    loop(PER // GROUP, GROUPS - 1, result_step)
    for i in range(GROUP):
        piece = hr.at[core, CHUNKS - 1, :, pl.ds(PER - GROUP + i, 1)]
        landed(piece, r_recv.at[GROUPS - 1 + i])
        result_forward(piece, CHUNKS - 1).start()

    left(ws.at[:, pl.ds(0, NE - 1)], w_send.at[0])
    left(ws.at[:, pl.ds(0, NE - 1)], r_send.at[0])
    left(wr.at[pl.ds(0, 3)], y_send.at[0])
    left(tr.at[core], tf_send.at[0])
    for n in range(CHUNKS):
        for h in range(2):
            left(ps.at[n, h], p_send.at[n, h])
    left(hr.at[core], rf_send.at[0])
    landed(hr.at[1 - core, CHUNKS - 1], rf_recv.at[CHUNKS - 1])


def finish(hr, table, part_out, out_hbm, grad_hbm, out_buf, grad_buf, sem):
    n_tok = out_buf.shape[0]
    last = CHUNKS - 1
    copies = []
    for b in range(4):
        half, h = b // 2, b % 2
        source = hr.at[half, last, pl.ds(h, 2)].reshape(2 * 8 * PER, COLS)
        for c in range(COLS // STEP):
            cols = slice(c * STEP, (c + 1) * STEP)
            total = dot(table[last, h], source[:, cols]) + part_out[b, :, cols].astype(F32)
            value = total.astype(BF)
            at = slice(b * COLS + c * STEP, b * COLS + (c + 1) * STEP)
            out_buf[:, at] = value[:n_tok]
            grad_buf[:, at] = value[n_tok:]
            for k, (buf, hbm) in enumerate(((out_buf, out_hbm), (grad_buf, grad_hbm))):
                copy = pltpu.make_async_copy(buf.at[:, at], hbm.at[:, at], sem.at[len(copies)])
                copy.start()
                copies.append(copy)
    for copy in copies:
        copy.wait()


def per_device(tokens, cotangent, routes, cluster, w_gate, w_up, w_down):
    n_tok, width = tokens.shape
    rows_dev = w_gate.shape[0]
    dma = pltpu.SemaphoreType.DMA
    rows = CAP * PER
    vmem = pl.BlockSpec(memory_space=pltpu.VMEM)
    results, table, settled = pl.pallas_call(
        kernel,
        out_shape=(
            pltpu.VMEM((2, CHUNKS, TILES, PER, 8, COLS), BF),
            pltpu.VMEM((CHUNKS, 2, 2 * n_tok, 2 * 8 * PER), BF),
            pltpu.VMEM((4, 2 * n_tok, COLS), BF),
        ),
        in_specs=[pl.BlockSpec(memory_space=pltpu.HBM)] * 7,
        out_specs=(vmem, vmem, vmem),
        scratch_shapes=[
            pltpu.VMEM((n_tok, width), BF),
            pltpu.VMEM((n_tok, width), BF),
            pltpu.VMEM((1, n_tok), jnp.int32),
            pltpu.VMEM(cluster.shape, jnp.int32),
            pltpu.VMEM((3, rows_dev, w_gate.shape[1]), BF),
            pltpu.VMEM((NE * 8, rows_dev), F32),
            pltpu.VMEM((3, NE, 8, COLS), BF),
            pltpu.VMEM((NDP, 3, NE, 8, COLS), BF),
            pltpu.VMEM((TILES, NE, 8, COLS), BF),
            pltpu.VMEM((2, CHUNKS, TILES, PER, 8, COLS), BF),
            pltpu.VMEM((4, 2 * rows, COLS), BF),
            pltpu.VMEM((rows, 3 * NE * 8), F32),
            pltpu.VMEM((CHUNKS, 2, 2 * rows, COLS), BF),
            pltpu.VMEM((CHUNKS, 2, 2 * rows, COLS), BF),
            pltpu.VMEM((2, 2 * rows, COLS), BF),
            pltpu.VMEM((4 * rows, COLS), BF),
            pltpu.VMEM((CHUNKS, TILES, PER, 8, COLS), BF),
            pltpu.VMEM((2, 2 * rows, 2 * 8 * PER), BF),
            pltpu.VMEM((TILES, 8 * PER, 2 * rows), BF),
            dma((7,)),
            dma((4,)),
            dma((1,)),
            dma((GROUPS,)),
            dma((1,)),
            dma((3, GROUPS)),
            dma((1,)),
            dma((GROUPS,)),
            dma((1,)),
            dma((CHUNKS,)),
            dma((CHUNKS, 2)),
            dma((CHUNKS, 2)),
            dma((1,)),
            dma((GROUPS - 1 + GROUP,)),
            dma((1,)),
            dma((CHUNKS,)),
        ],
        compiler_params=pltpu.CompilerParams(
            collective_id=0, has_side_effects=True, vmem_limit_bytes=VMEM_BYTES
        ),
    )(tokens, cotangent, routes.reshape(1, n_tok), cluster, w_gate, w_up, w_down)
    shape = jax.ShapeDtypeStruct((n_tok, width), BF)
    hbm = pl.BlockSpec(memory_space=pltpu.HBM)
    return pl.pallas_call(
        finish,
        out_shape=(shape, shape),
        in_specs=[vmem, vmem, vmem],
        out_specs=(hbm, hbm),
        scratch_shapes=[
            pltpu.VMEM((n_tok, width), BF),
            pltpu.VMEM((n_tok, width), BF),
            dma((2 * width // STEP,)),
        ],
        compiler_params=pltpu.CompilerParams(vmem_limit_bytes=16 << 20),
    )(results, table, settled)


def solution(mesh):
    in_specs = (
        P(("dp", "expert"), None),
        P(("dp", "expert"), None),
        P(("dp", "expert"), None),
        P(),
        P(("expert", "tensor"), "dp"),
        P(("expert", "tensor"), "dp"),
        P(("expert", "tensor"), "dp"),
    )
    out_specs = (P(("dp", "expert"), None), P(("dp", "expert"), None))
    return jax.shard_map(
        per_device, mesh=mesh, in_specs=in_specs, out_specs=out_specs, check_vma=False
    )
```
